256 devices in a mesh: rows: 256 (over x, y, z, core).
Axes of the slice: x: 4, y: 4, z: 8, core: 2. Of those that a mesh axis runs over, the one named last changes fastest.
Arguments:
- hamiltonian: float32 [393216, 1728], P('rows'), may hold values from -0.15625 to 0.15625
- subspace: float32 [393216, 128], P('rows'), may hold values from -6 to 6
- block_cols: int32 [6144, 27], P('rows'), may hold values from 0 to 6151, as said below
- far_list: int32 [256, 8], P('rows'), may hold values from -1 to 6143, as said below
Outputs:
- filtered: float32 [393216, 128], P('rows')
The draws below stay inside these ranges and needn't reach their ends.
Inputs may be any that keep to these rules, and one draw needn't show every extreme that they name: `far_list`: row d holds in slots 0 to c_d - 1 distinct block indices owned by device d xor (32) (that device owns blocks k * 24 to k * 24 + 23 for its index k), and -1 in its other slots; c_d is 2 or more, and device 0 fills all 8 slots. `block_cols`: entry 0 of row i is i; the next 24 entries are distinct blocks (i + o) mod 6144 with 0 < |o| <= 13; the last two are 6144 + s for two distinct filled slots s of far_list's row of the device that owns row i.
All inputs are finite; a program needn't handle non-finite values.
Results may differ from the reference program's by a relative error of at most 0.000058.
Values sent between devices are 32-bit elements; how exact they have to be, the bound alone decides.
A program may use at most 128 MiB of HBM per device.

```python
import jax
import jax.numpy as jnp
from jax import lax

B = 64
K = 128
REACH = 13
NBD = 24
NNZ = 27
M = 8
NROW = 393216
N_ROWS = 256


def layout(key):
    folded = jax.random.fold_in(key, 7)
    subkeys = jax.random.split(folded, 7)
    block_total = NBD * N_ROWS
    device = jnp.arange(N_ROWS, dtype=jnp.int32)
    partner = jnp.bitwise_xor(device, N_ROWS // 8)
    crowded = jax.random.randint(subkeys[0], (N_ROWS,), 0, 20) < 3
    sparse_count = jax.random.randint(subkeys[1], (N_ROWS,), 2, max(3, M // 3 + 1))
    filled = jnp.where(crowded | (device == 0), M, sparse_count).astype(jnp.int32)
    scores = jax.random.randint(subkeys[2], (N_ROWS, NBD), 0, 1 << 20) * NBD + jnp.arange(NBD, dtype=jnp.int32)[None, :]
    chosen = jnp.argsort(scores, axis=1)[:, :M].astype(jnp.int32)
    slot_ids = jnp.arange(M, dtype=jnp.int32)[None, :]
    far_list = jnp.where(slot_ids < filled[:, None], partner[:, None] * NBD + chosen, -1).astype(jnp.int32)
    row_index = jnp.arange(block_total, dtype=jnp.int32)
    owner_device = row_index // NBD
    span = 2 * REACH
    first_drop = jax.random.randint(subkeys[3], (block_total,), 0, span)
    second_drop = (first_drop + 1 + jax.random.randint(subkeys[4], (block_total,), 0, span - 1)) % span
    offset_index = jnp.arange(span, dtype=jnp.int32)[None, :]
    dropped = (offset_index == first_drop[:, None]) | (offset_index == second_drop[:, None])
    keeping = jnp.argsort(offset_index + 4 * REACH * dropped.astype(jnp.int32), axis=1)[:, :span - 2]
    offsets_all = jnp.concatenate([jnp.arange(-REACH, 0, dtype=jnp.int32), jnp.arange(1, REACH + 1, dtype=jnp.int32)])
    kept_offsets = offsets_all[keeping]
    with_self = jnp.concatenate([jnp.zeros((block_total, 1), jnp.int32), kept_offsets], axis=1)
    banded = (row_index[:, None] + with_self) % block_total
    slot_count = filled[owner_device]
    first_slot = jax.random.randint(subkeys[5], (block_total,), 0, slot_count)
    second_slot = (first_slot + 1 + jax.random.randint(subkeys[6], (block_total,), 0, slot_count - 1)) % slot_count
    block_cols = jnp.concatenate([banded, (block_total + first_slot)[:, None], (block_total + second_slot)[:, None]], axis=1)
    return (far_list, block_cols.astype(jnp.int32))


def draw_block_cols(key, part):
    return layout(key)[1]


def draw_far_list(key, part):
    return layout(key)[0]


def steps_of(rng, dims, pieces, least, largest):
    level, own = 1.0, jax.random.fold_in(rng, 6)
    for position, blocks in pieces:
        steps = jnp.exp(jax.random.uniform(jax.random.fold_in(own, position), (blocks,), jnp.float32, least / len(pieces), largest / len(pieces)))
        level = level * jnp.repeat(steps, dims[position] // blocks).reshape([-1 if axis == position else 1 for axis in range(len(dims))])
    return level


def bell_draw(rng, extent, deviation, bound, cuts=(), held_as=jnp.bfloat16):
    values = jax.random.normal(rng, extent, jnp.float32) * deviation
    if len(cuts) > 0:
        values = steps_of(rng, extent, cuts, -0.22, 0.18) * values
    return jnp.clip(values, min=-bound, max=bound).astype(held_as)


def setup_inputs(seed: int = 0) -> dict:
    seeds = jax.random.split(jax.random.key(seed), 5)
    hamiltonian = bell_draw(seeds[0], (NROW, NNZ * B), (NNZ * B) ** -0.5, 0.15625, ((0, 256),), jnp.float32)
    subspace = bell_draw(seeds[1], (NROW, K), 1.0, 6.0, ((0, 256),), jnp.float32)
    block_cols = draw_block_cols(jax.random.fold_in(seeds[4], 71), 0)
    far_list = draw_far_list(jax.random.fold_in(seeds[4], 71), 0)
    return dict(hamiltonian=hamiltonian, subspace=subspace, block_cols=block_cols, far_list=far_list)


CENTER = 0.25
HALF_WIDTH = 1.5


def resolve(block_cols, far_list):
    block_total = NBD * N_ROWS
    owner_row = (jnp.arange(block_total, dtype=jnp.int32) // NBD)[:, None]
    slot_index = jnp.clip(block_cols - block_total, 0, M - 1).astype(jnp.int32)
    remote = far_list[owner_row, slot_index]
    return jnp.where(block_cols < block_total, block_cols, remote).astype(jnp.int32)


def apply_operator(hamiltonian, vectors, columns):
    blocks = vectors.reshape(N_ROWS * NBD, B, K)
    ham_slabs = hamiltonian.reshape(N_ROWS, NBD, B, NNZ * B)
    col_slabs = columns.reshape(N_ROWS, NBD, NNZ)

    def product_slab(operands):
        ham_slab, cols_slab = operands
        picked = blocks[cols_slab].reshape(NBD, NNZ * B, K)
        return jnp.einsum("irm,imk->irk", ham_slab, picked, precision=lax.Precision.HIGHEST)

    result = lax.map(product_slab, (ham_slabs, col_slabs))
    return result.reshape(N_ROWS * NBD * B, K)


def reference(hamiltonian, subspace, block_cols, far_list):
    columns = resolve(block_cols, far_list)
    first_term = (apply_operator(hamiltonian, subspace, columns) - CENTER * subspace) / HALF_WIDTH
    second = apply_operator(hamiltonian, first_term, columns)
    return (2.0 / HALF_WIDTH) * (second - CENTER * first_term) - subspace
```

```python
import functools

import jax
import jax.numpy as jnp
from jax import lax
from jax.experimental import pallas as pl
from jax.experimental.pallas import tpu as pltpu
from jax.sharding import PartitionSpec as P

CENTER = 0.25
HALF_WIDTH = 1.5
REACH = 13
ROWS_PER_STEP = 4


def partner(value, axis, bit):
    mask = 2**bit
    pairs = [(source, source ^ mask) for source in range(lax.axis_size(axis))]
    return lax.ppermute(value, axis, pairs)


def halo(value, axis, width):
    devices, length = lax.axis_size(axis), value.shape[0]
    up = [(i, (i + 1) % devices) for i in range(devices)]
    down = [(j, i) for i, j in up]
    before = lax.ppermute(value[length - width:], axis, up)
    after = lax.ppermute(value[:width], axis, down)
    return before, after


def apply_kernel(mode, entries, block_size, pos_ref, ham_ref, ext_ref, own_ref, *rest):
    if mode == 0:
        (out_ref,) = rest
    else:
        base_ref, out_ref = rest
    step = pl.program_id(0)
    rows = ham_ref.shape[0] // block_size
    for r in range(rows):
        i = step * rows + r
        pieces = []
        for j in range(entries):
            start = pl.multiple_of(pos_ref[i * entries + j] * block_size, block_size)
            pieces.append(ext_ref[pl.ds(start, block_size), :])
        panel = jnp.concatenate(pieces, axis=0)
        acc = jnp.dot(
            ham_ref[r * block_size:(r + 1) * block_size, :],
            panel,
            precision=lax.Precision.HIGHEST,
            preferred_element_type=jnp.float32,
        )
        rs = slice(r * block_size, (r + 1) * block_size)
        own = own_ref[rs, :]
        if mode == 0:
            out_ref[rs, :] = (acc - CENTER * own) / HALF_WIDTH
        else:
            out_ref[rs, :] = 2.0 / HALF_WIDTH * (acc - CENTER * own) - base_ref[rs, :]


def block_apply(mode, entries, positions, hamiltonian, extended, own, base=None):
    block_size = hamiltonian.shape[1] // entries
    block_rows = own.shape[0] // block_size
    step_rows = ROWS_PER_STEP * block_size
    steps = block_rows // ROWS_PER_STEP
    width = own.shape[1]
    in_specs = [
        pl.BlockSpec((step_rows, hamiltonian.shape[1]), lambda s, pos: (s, 0)),
        pl.BlockSpec(extended.shape, lambda s, pos: (0, 0)),
        pl.BlockSpec((step_rows, width), lambda s, pos: (s, 0)),
    ]
    args = [hamiltonian, extended, own]
    if mode == 1:
        in_specs.append(pl.BlockSpec((step_rows, width), lambda s, pos: (s, 0)))
        args.append(base)
    flops = 2 * hamiltonian.shape[0] * hamiltonian.shape[1] * width
    return pl.pallas_call(
        functools.partial(apply_kernel, mode, entries, block_size),
        out_shape=jax.ShapeDtypeStruct(own.shape, jnp.float32),
        grid_spec=pltpu.PrefetchScalarGridSpec(
            num_scalar_prefetch=1,
            grid=(steps,),
            in_specs=in_specs,
            out_specs=pl.BlockSpec((step_rows, width), lambda s, pos: (s, 0)),
        ),
        compiler_params=pltpu.CompilerParams(vmem_limit_bytes=48 * 1024 * 1024),
        cost_estimate=pl.CostEstimate(
            flops=6 * flops,
            transcendentals=0,
            bytes_accessed=4 * (hamiltonian.size + extended.size + 3 * own.size),
        ),
    )(positions, *args)


def per_device(hamiltonian, subspace, block_cols, far_list):
    block_rows, entries = block_cols.shape
    block_size = hamiltonian.shape[1] // entries
    sub_width = subspace.shape[1]
    slot_total = far_list.shape[1]
    device_count = lax.axis_size("rows")
    my_index = lax.axis_index("rows")
    block_total = block_rows * device_count
    swap_level = (device_count // 8).bit_length() - 1
    first_row = my_index * block_rows
    inband = block_cols < block_total
    slot_index = jnp.clip(block_cols - block_total, 0, slot_total - 1)
    asked_list = partner(far_list, "rows", swap_level)
    valid_mask = (asked_list[0] >= 0).astype(jnp.float32)
    local_index = jnp.clip(asked_list[0] - first_row, 0, block_rows - 1)
    band_count = block_rows + 2 * REACH
    positions = jnp.where(
        inband, (block_cols - first_row + REACH) % block_total, band_count + slot_index
    )
    positions = jnp.clip(positions, 0, band_count + slot_total - 1).reshape(-1)
    halo_rows = REACH * block_size

    def extend(vectors):
        before, after = halo(vectors, "rows", halo_rows)
        outgoing = (
            vectors.reshape(block_rows, block_size, sub_width)[local_index]
            * valid_mask[:, None, None]
        )
        remote = partner(outgoing.reshape(slot_total * block_size, sub_width), "rows", swap_level)
        return jnp.concatenate([before, vectors, after, remote], axis=0)

    first_term = block_apply(0, entries, positions, hamiltonian, extend(subspace), subspace)
    return block_apply(1, entries, positions, hamiltonian, extend(first_term), first_term, subspace)


def solution(mesh):
    placed = (P("rows", None), P("rows", None), P("rows", None), P("rows", None))
    return jax.shard_map(
        per_device, mesh=mesh, in_specs=placed, out_specs=P("rows", None), check_vma=False
    )
```

```python
import functools

import jax
import jax.numpy as jnp
from jax import lax
from jax.experimental import pallas as pl
from jax.experimental.pallas import tpu as pltpu
from jax.sharding import PartitionSpec as P

CENTER = 0.25
HALF_WIDTH = 1.5
REACH = 13
ROWS_PER_STEP = 4


def partner(value, axis, bit):
    mask = 2**bit
    pairs = [(source, source ^ mask) for source in range(lax.axis_size(axis))]
    return lax.ppermute(value, axis, pairs)


def halo(value, axis, width):
    devices, length = lax.axis_size(axis), value.shape[0]
    up = [(i, (i + 1) % devices) for i in range(devices)]
    down = [(j, i) for i, j in up]
    before = lax.ppermute(value[length - width:], axis, up)
    after = lax.ppermute(value[:width], axis, down)
    return before, after


def split(x):
    hi = x.astype(jnp.bfloat16)
    return hi, (x - hi.astype(jnp.float32)).astype(jnp.bfloat16)


def split_dot(transposed, panel):
    numbers = (((0,), (0,)), ((), ()))
    th, tl = split(transposed)
    ph, pw = split(panel)

    def dot(a, b):
        return lax.dot_general(a, b, numbers, preferred_element_type=jnp.float32)

    return dot(th, ph) + (dot(th, pw) + dot(tl, ph))


def apply_kernel(mode, entries, block_size, pos_ref, ham_ref, ext_ref, own_ref, *rest):
    if mode == 0:
        (out_ref,) = rest
    else:
        base_ref, out_ref = rest
    step = pl.program_id(0)
    rows = ham_ref.shape[1] // block_size
    for r in range(rows):
        i = step * rows + r
        pieces = []
        for j in range(entries):
            start = pl.multiple_of(pos_ref[i * entries + j] * block_size, block_size)
            pieces.append(ext_ref[pl.ds(start, block_size), :])
        panel = jnp.concatenate(pieces, axis=0)
        acc = split_dot(ham_ref[:, r * block_size:(r + 1) * block_size], panel)
        rs = slice(r * block_size, (r + 1) * block_size)
        own = own_ref[rs, :]
        if mode == 0:
            out_ref[rs, :] = (acc - CENTER * own) / HALF_WIDTH
        else:
            out_ref[rs, :] = 2.0 / HALF_WIDTH * (acc - CENTER * own) - base_ref[rs, :]


def block_apply(mode, entries, positions, transposed, extended, own, base=None):
    block_size = transposed.shape[0] // entries
    block_rows = own.shape[0] // block_size
    step_rows = ROWS_PER_STEP * block_size
    steps = block_rows // ROWS_PER_STEP
    width = own.shape[1]
    in_specs = [
        pl.BlockSpec((transposed.shape[0], step_rows), lambda s, pos: (0, s)),
        pl.BlockSpec(extended.shape, lambda s, pos: (0, 0)),
        pl.BlockSpec((step_rows, width), lambda s, pos: (s, 0)),
    ]
    args = [transposed, extended, own]
    if mode == 1:
        in_specs.append(pl.BlockSpec((step_rows, width), lambda s, pos: (s, 0)))
        args.append(base)
    flops = 2 * transposed.shape[0] * transposed.shape[1] * width
    return pl.pallas_call(
        functools.partial(apply_kernel, mode, entries, block_size),
        out_shape=jax.ShapeDtypeStruct(own.shape, jnp.float32),
        grid_spec=pltpu.PrefetchScalarGridSpec(
            num_scalar_prefetch=1,
            grid=(steps,),
            in_specs=in_specs,
            out_specs=pl.BlockSpec((step_rows, width), lambda s, pos: (s, 0)),
        ),
        compiler_params=pltpu.CompilerParams(vmem_limit_bytes=48 * 1024 * 1024),
        cost_estimate=pl.CostEstimate(
            flops=3 * flops,
            transcendentals=0,
            bytes_accessed=4 * (transposed.size + extended.size + 3 * own.size),
        ),
    )(positions, *args)


def per_device(hamiltonian, subspace, block_cols, far_list):
    block_rows, entries = block_cols.shape
    block_size = hamiltonian.shape[1] // entries
    sub_width = subspace.shape[1]
    slot_total = far_list.shape[1]
    device_count = lax.axis_size("rows")
    my_index = lax.axis_index("rows")
    block_total = block_rows * device_count
    swap_level = (device_count // 8).bit_length() - 1
    first_row = my_index * block_rows
    inband = block_cols < block_total
    slot_index = jnp.clip(block_cols - block_total, 0, slot_total - 1)
    asked_list = partner(far_list, "rows", swap_level)
    valid_mask = (asked_list[0] >= 0).astype(jnp.float32)
    local_index = jnp.clip(asked_list[0] - first_row, 0, block_rows - 1)
    band_count = block_rows + 2 * REACH
    positions = jnp.where(
        inband, (block_cols - first_row + REACH) % block_total, band_count + slot_index
    )
    positions = jnp.clip(positions, 0, band_count + slot_total - 1).reshape(-1)
    halo_rows = REACH * block_size

    def extend(vectors):
        before, after = halo(vectors, "rows", halo_rows)
        outgoing = (
            vectors.reshape(block_rows, block_size, sub_width)[local_index]
            * valid_mask[:, None, None]
        )
        remote = partner(outgoing.reshape(slot_total * block_size, sub_width), "rows", swap_level)
        return jnp.concatenate([before, vectors, after, remote], axis=0)

    transposed = hamiltonian.T
    first_term = block_apply(0, entries, positions, transposed, extend(subspace), subspace)
    return block_apply(1, entries, positions, transposed, extend(first_term), first_term, subspace)


def solution(mesh):
    placed = (P("rows", None), P("rows", None), P("rows", None), P("rows", None))
    return jax.shard_map(
        per_device, mesh=mesh, in_specs=placed, out_specs=P("rows", None), check_vma=False
    )
```
